1024 devices in a mesh: grp: 8 (over y), col: 128 (over z, x, core).
Axes of the slice: x: 4, y: 8, z: 16, core: 2. Of those that a mesh axis runs over, the one named last changes fastest.
Arguments:
- doc_factors: float32 [4096, 256], P(('grp', 'col')), may hold values from -1.5 to 1.5
- ngram_factors: float32 [65536, 256], P('col'), may hold values from -1.5 to 1.5
- block_docs: int32 [8, 128, 16], P('grp', 'col'), may hold values from 0 to 3, as said below
- block_ngrams: int32 [8, 128, 16], P('grp', 'col'), may hold values from 0 to 3, as said below
- block_counts: int32 [8, 128], P('grp', 'col'), may hold values from 4 to 16, as said below
- pmi: bfloat16 [8, 128, 16, 128, 128], P('grp', 'col'), may hold values from -6 to 6
- weights: bfloat16 [8, 128, 16, 128, 128], P('grp', 'col'), may hold values from 0.049804688 to 1
Outputs:
- doc_out: float32 [4096, 256], P(('grp', 'col'))
- ngram_out: float32 [65536, 256], P('col')
The draws below stay inside these ranges and needn't reach their ends.
Inputs may be any that keep to these rules, and one draw needn't show every extreme that they name: `block_docs`: within one device's slots every pair (document block, n-gram block) appears exactly once. `block_ngrams`: paired with block_docs as stated there. `block_counts`: some device has all 16 slots live.
All inputs are finite; a program needn't handle non-finite values.
Results may differ from the reference program's by a relative error of at most 0.0086.
Values may be sent and summed in bfloat16 or wider, within the bound.
A program may use at most 32 MiB of HBM per device.

```python
import math
import jax
import jax.numpy as jnp
from jax import lax

R = 256
BLK = 128
DBG = 4
NGB = 4
CAP = 16
GROUPS = 8
SHARDS = 128
NDOC = 4096
NNG = 65536
N_GRP = 8
N_COL = 128


def pair_table(key):
    keys = jax.random.split(jax.random.fold_in(key, 7), GROUPS * SHARDS)
    orders = jax.vmap(lambda one: jax.random.permutation(one, CAP))(keys)
    return orders.reshape(GROUPS, SHARDS, CAP).astype(jnp.int32)


def draw_block_docs(key, part):
    return (pair_table(key) // NGB).astype(jnp.int32)


def draw_block_ngrams(key, part):
    return (pair_table(key) % NGB).astype(jnp.int32)


def draw_block_counts(key, part):
    spread = jax.random.randint(jax.random.fold_in(key, 11), (GROUPS * SHARDS,), 0, CAP - 3)
    counts = 4 + spread * spread // (CAP - 4)
    chosen = jax.random.randint(jax.random.fold_in(key, 12), (), 0, GROUPS * SHARDS)
    counts = counts.at[chosen].set(CAP)
    return counts.reshape(GROUPS, SHARDS).astype(jnp.int32)


def draw_doc_factors(key, part):
    first = jax.random.fold_in(key, 31)
    values = 0.25 * jax.random.normal(first, (NDOC, R), jnp.float32)
    return jnp.clip(values, -1.5, 1.5).astype(jnp.float32)


def draw_ngram_factors(key, part):
    first = jax.random.fold_in(key, 41)
    values = 0.25 * jax.random.normal(first, (NNG, R), jnp.float32)
    return jnp.clip(values, -1.5, 1.5).astype(jnp.float32)


def block_levels(own_key, extent, shards, least, high):
    gain, own = 1.0, jax.random.fold_in(own_key, 6)
    for axis_at, shards_of in shards:
        heights = jnp.exp(jax.random.uniform(jax.random.fold_in(own, axis_at), (shards_of,), jnp.float32, least / len(shards), high / len(shards)))
        gain = gain * jnp.repeat(heights, extent[axis_at] // shards_of).reshape([-1 if axis == axis_at else 1 for axis in range(len(extent))])
    return gain


def normal_values(key, dims, deviation, most, cuts=(), kind=jnp.bfloat16):
    drawn = deviation * jax.random.normal(key, dims, jnp.float32)
    if cuts:
        drawn = drawn * block_levels(key, dims, cuts, -0.22, 0.18)
    return jnp.clip(drawn, -most, most).astype(kind)


def setup_inputs(seed: int = 0) -> dict:
    key_of = jax.random.split(jax.random.key(seed), 8)
    doc_factors = draw_doc_factors(jax.random.fold_in(key_of[7], 71), 0)
    ngram_factors = draw_ngram_factors(jax.random.fold_in(key_of[7], 71), 0)
    block_docs = draw_block_docs(jax.random.fold_in(key_of[7], 71), 0)
    block_ngrams = draw_block_ngrams(jax.random.fold_in(key_of[7], 71), 0)
    block_counts = draw_block_counts(jax.random.fold_in(key_of[7], 71), 0)
    pmi = normal_values(key_of[5], (GROUPS, SHARDS, CAP, BLK, BLK), 1.0, 6.0, ((0, 8), (1, 128)))
    weights = jnp.clip(jnp.exp(math.log(1.0) - 2.9996462 * jax.random.uniform(key_of[6], (GROUPS, SHARDS, CAP, BLK, BLK), jnp.float32) ** block_levels(key_of[6], (GROUPS, SHARDS, CAP, BLK, BLK), ((0, 8), (1, 128)), -0.2, 0.2)), 0.049804688, 1.0).astype(jnp.bfloat16)
    return dict(doc_factors=doc_factors, ngram_factors=ngram_factors, block_docs=block_docs, block_ngrams=block_ngrams, block_counts=block_counts, pmi=pmi, weights=weights)


def gradients(doc_now, ngram_now, block_docs, block_ngrams, block_counts, pmi, weights):
    highest = lax.Precision.HIGHEST
    doc_half = lax.optimization_barrier(doc_now.astype(jnp.bfloat16))
    ngram_half = lax.optimization_barrier(ngram_now.astype(jnp.bfloat16))
    doc_blocks = doc_half.reshape(N_GRP * DBG, BLK, R)
    ngram_blocks = ngram_half.reshape(N_COL * NGB, BLK, R)
    slots = jnp.arange(CAP, dtype=jnp.int32)
    total = N_GRP * N_COL
    group_ids = (jnp.arange(total, dtype=jnp.int32) // N_COL).astype(jnp.int32)
    shard_ids = (jnp.arange(total, dtype=jnp.int32) % N_COL).astype(jnp.int32)

    def visit(carry, item):
        grad_doc, grad_ngram = carry
        docs, ngrams, count, tiles, scales, group, shard = item
        doc_ids = (group * DBG + docs).astype(jnp.int32)
        ngram_ids = (shard * NGB + ngrams).astype(jnp.int32)
        left = doc_blocks[doc_ids].astype(jnp.float32)
        right = ngram_blocks[ngram_ids].astype(jnp.float32)
        scores = jnp.einsum('kir,kjr->kij', left, right, precision=highest)
        live = (slots < count).astype(jnp.float32)
        err = (live[:, None, None] * scales.astype(jnp.float32) * (scores - tiles.astype(jnp.float32))).astype(jnp.bfloat16)
        err = lax.optimization_barrier(err).astype(jnp.float32)
        grad_doc = grad_doc.at[doc_ids].add(jnp.einsum('kij,kjr->kir', err, right, precision=highest))
        grad_ngram = grad_ngram.at[ngram_ids].add(jnp.einsum('kij,kir->kjr', err, left, precision=highest))
        return ((grad_doc, grad_ngram), None)
    start = (jnp.zeros((N_GRP * DBG, BLK, R), jnp.float32), jnp.zeros((N_COL * NGB, BLK, R), jnp.float32))
    items = (block_docs.reshape(total, CAP), block_ngrams.reshape(total, CAP), block_counts.reshape(total), pmi.reshape(total, CAP, BLK, BLK), weights.reshape(total, CAP, BLK, BLK), group_ids, shard_ids)
    (grad_doc, grad_ngram), unused = lax.scan(visit, start, items)
    return (grad_doc.reshape(doc_now.shape), grad_ngram.reshape(ngram_now.shape))

def reference(doc_factors, ngram_factors, block_docs, block_ngrams, block_counts, pmi, weights):
    doc_base = math.sqrt(NNG) + 1.5 * math.sqrt(R)
    ngram_base = math.sqrt(NDOC) + 1.5 * math.sqrt(R)
    doc_rate = 100.0 / (doc_base * doc_base)
    ngram_rate = 100.0 / (ngram_base * ngram_base)
    doc_now = doc_factors
    ngram_now = ngram_factors
    for step in range(2):
        grad_doc, grad_ngram = gradients(doc_now, ngram_now, block_docs, block_ngrams, block_counts, pmi, weights)
        doc_now = doc_now - doc_rate * grad_doc
        ngram_now = ngram_now - ngram_rate * grad_ngram
    return (doc_now, ngram_now)
```

```python
import functools
import math

import jax
import jax.numpy as jnp
from jax import lax
from jax.experimental import pallas as pl
from jax.experimental.pallas import tpu as pltpu
from jax.sharding import PartitionSpec as P

MESH = pl.DeviceIdType.MESH
F32 = jnp.float32
BF16 = jnp.bfloat16
CORES = 2
PLANE = 8
CHUNKS = 4
NT = (((1,), (1,)), ((), ()))
TN = (((0,), (0,)), ((), ()))


def hop(p, n):
    return n // 2 + ((p + 1) // 2) * (1 - 2 * (p % 2))


def kernel(
    Z,
    Q,
    G,
    doc_rate,
    ngram_rate,
    doc_ref,
    docs_ref,
    ngrams_ref,
    count_ref,
    ngram_hbm,
    pmi_hbm,
    weights_hbm,
    doc_out,
    ngram_out,
    v32,
    tiles,
    scales,
    v16,
    u16,
    dense_p,
    dense_w,
    err,
    slot_of,
    own32,
    swap_out,
    swap_in,
    gath,
    xs,
    xr,
    rsum,
    zs,
    zr,
    ys,
    yr,
    yg,
    load_sem,
    swap_send,
    swap_recv,
    agz_send,
    agz_recv,
    agx_send,
    agx_recv,
    rsx_send,
    rsx_recv,
    rsz_send,
    rsz_recv,
    ys_send,
    ys_recv,
    yg_send,
    yg_recv,
):
    X = Q // CORES
    rows = 8 * X
    per = Z // CHUNKS
    chunk_rows = per * rows
    half = doc_ref.shape[1] // 2
    nslots, block_rows, block_cols = tiles.shape
    nnb = v32.shape[0] // block_cols
    per_block = block_rows // rows
    piece = v32.shape[0] // G

    g = lax.axis_index("grp")
    col = lax.axis_index("col")
    z = col // Q
    q = col % Q
    core = q % CORES
    partner = q + 1 - 2 * core

    def at_z(dz):
        return {"col": ((z + dz) % Z) * Q + q}

    def at_q(r):
        return {"col": z * Q + (q + r) % Q}

    def at_g(r):
        return {"grp": (g + r) % G}

    loads = [
        pltpu.make_async_copy(ngram_hbm, v32, load_sem.at[0]),
        pltpu.make_async_copy(pmi_hbm, tiles, load_sem.at[1]),
        pltpu.make_async_copy(weights_hbm, scales, load_sem.at[2]),
    ]
    for load in loads:
        load.start()

    barrier = pltpu.get_barrier_semaphore()

    @pl.loop(1, Z)
    def _(d):
        pl.semaphore_signal(barrier, inc=1, device_id=at_z(d), device_id_type=MESH)

    @pl.loop(1, Q)
    def _(d):
        pl.semaphore_signal(barrier, inc=1, device_id=at_q(d), device_id_type=MESH)

    @pl.loop(1, G)
    def _(d):
        pl.semaphore_signal(barrier, inc=1, device_id=at_g(d), device_id_type=MESH)

    @pl.loop(0, nslots)
    def _(pair):
        found = jnp.int32(0)
        for k in range(nslots):
            name = docs_ref[0, 0, k] * nnb + ngrams_ref[0, 0, k]
            found = jnp.maximum(found, jnp.where(name == pair, k, 0))
        slot_of[pair] = found

    count = count_ref[0, 0]
    for load in loads:
        load.wait()

    v16[...] = v32[...].astype(BF16)

    @pl.loop(0, Z)
    def _(p):
        zd = (z + hop(p, Z)) % Z
        block = zd // per_block
        first = pl.multiple_of((zd % per_block) * rows, rows)
        to = pl.multiple_of(p * rows, rows)
        for n in range(nnb):
            k = slot_of[block * nnb + n]
            lanes = slice(n * block_cols, (n + 1) * block_cols)
            live = jnp.where(k < count, 1.0, 0.0).astype(F32)
            dense_p[pl.ds(to, rows), lanes] = tiles[k, pl.ds(first, rows), :]
            dense_w[pl.ds(to, rows), lanes] = (
                live * scales[k, pl.ds(first, rows), :].astype(F32)
            ).astype(BF16)

    is_low = core == 0
    low = doc_ref[:, :half]
    high = doc_ref[:, half:]
    swap_out[0] = jnp.where(is_low, high, low)

    pl.semaphore_wait(barrier, Z + Q + G - 3)

    def swap(turn):
        return pltpu.make_async_remote_copy(
            src_ref=swap_out.at[turn],
            dst_ref=swap_in.at[turn],
            send_sem=swap_send.at[turn],
            recv_sem=swap_recv.at[turn],
            device_id={"col": z * Q + partner},
            device_id_type=MESH,
        )

    first_swap = swap(0)
    first_swap.start()
    mine = jnp.where(is_low, low, high)
    first_swap.wait()
    other = swap_in[0]
    own32[0:4, :] = jnp.where(is_low, mine, other)
    own32[4:8, :] = jnp.where(is_low, other, mine)

    def settle(ref, sem):
        pltpu.make_async_copy(ref, ref, sem).wait()

    def gather_documents(step, filler):
        here = gath.at[step]
        here[z, q] = own32[...].astype(BF16)

        def along_z(p):
            return pltpu.make_async_remote_copy(
                src_ref=here.at[z, q],
                dst_ref=here.at[z, q],
                send_sem=agz_send.at[step],
                recv_sem=agz_recv.at[step, p],
                device_id=at_z(hop(p, Z)),
                device_id_type=MESH,
            )

        def forward(source):
            for r in range(1, Q):
                pltpu.make_async_remote_copy(
                    src_ref=here.at[source, q],
                    dst_ref=here.at[source, q],
                    send_sem=agx_send.at[step],
                    recv_sem=agx_recv.at[step, r],
                    device_id=at_q(r),
                    device_id_type=MESH,
                ).start()

        @pl.loop(0, Z - 1)
        def _(p):
            along_z(p).start()

        forward(z)

        @pl.loop(0, Z - 1)
        def _(i):
            p = Z - 2 - i
            source = (z + Z - hop(p, Z)) % Z
            settle(here.at[source, q], agz_recv.at[step, p])
            forward(source)

        filler()

        @pl.loop(1, Q)
        def _(r):
            settle(here.at[:, 0], agx_recv.at[step, r])

        @pl.loop(0, Z)
        def _(p):
            zd = (z + hop(p, Z)) % Z
            to = pl.multiple_of(p * rows, rows)
            for c in range(CORES):
                parts = [here[zd, x * CORES + c].astype(F32) for x in range(X)]
                u16[pl.ds(to, rows), c * half : (c + 1) * half] = jnp.concatenate(
                    parts, axis=0
                ).astype(BF16)

    def find_errors(ch):
        at = pl.ds(pl.multiple_of(ch * chunk_rows, chunk_rows), chunk_rows)
        scores = lax.dot_general(u16[at, :], v16[...], NT, preferred_element_type=F32)
        err[at, :] = (
            dense_w[at, :].astype(F32) * (scores - dense_p[at, :].astype(F32))
        ).astype(BF16)

    def send_documents(step, ch):
        at = pl.ds(pl.multiple_of(ch * chunk_rows, chunk_rows), chunk_rows)
        grad = jnp.dot(err[at, :], v16[...], preferred_element_type=F32)
        for k in range(per):
            for x in range(X):
                for c in range(CORES):
                    top = k * rows + x * 8
                    xs[step, x * CORES + c, ch * per + k] = grad[
                        top : top + 8, c * half : (c + 1) * half
                    ].astype(BF16)
        for r in range(1, Q):
            pltpu.make_async_remote_copy(
                src_ref=xs.at[step, (q + r) % Q, pl.ds(ch * per, per)],
                dst_ref=xr.at[step, r, pl.ds(ch * per, per)],
                send_sem=rsx_send.at[step],
                recv_sem=rsx_recv.at[step, ch, r],
                device_id=at_q(r),
                device_id_type=MESH,
            ).start()

    def send_ngrams(step):
        for n in range(nnb):
            grad = lax.dot_general(
                err[:, n * block_cols : (n + 1) * block_cols],
                u16[...],
                TN,
                preferred_element_type=F32,
            )
            for k in range(block_cols // piece):
                ys[step, n * (block_cols // piece) + k] = grad[
                    k * piece : (k + 1) * piece, :
                ].astype(BF16)
        for p in range(G - 1):
            r = hop(p, G)
            pltpu.make_async_remote_copy(
                src_ref=ys.at[step, (g + r) % G],
                dst_ref=yr.at[step, r],
                send_sem=ys_send.at[step],
                recv_sem=ys_recv.at[step, r],
                device_id=at_g(r),
                device_id_type=MESH,
            ).start()

    def reduce_plane(step):
        @pl.loop(0, CHUNKS)
        def _(ch):
            at = pl.ds(ch * per, per)
            total = xs[step, q, at].astype(F32)
            for r in range(1, Q):
                settle(xr.at[step, r, at], rsx_recv.at[step, ch, r])
            for r in range(1, Q):
                total = total + xr[step, r, at].astype(F32)
            rsum[step, at] = total
            zs[step, at] = total.astype(BF16)

            @pl.loop(0, per)
            def _(k):
                p = ch * per + k

                @pl.when(p < Z - 1)
                def _():
                    pltpu.make_async_remote_copy(
                        src_ref=zs.at[step, p],
                        dst_ref=zr.at[step, p],
                        send_sem=rsz_send.at[step],
                        recv_sem=rsz_recv.at[step, p],
                        device_id=at_z(hop(p, Z)),
                        device_id_type=MESH,
                    ).start()

    def update_documents(step):
        total = rsum[step, Z - 1]
        for p in range(Z - 1):
            settle(zr.at[step, p], rsz_recv.at[step, p])
        for p in range(Z - 1):
            total = total + zr[step, p].astype(F32)
        own32[...] = own32[...] - doc_rate * total

    def reduce_ngrams(step):
        for r in range(1, G):
            settle(yr.at[step, r], ys_recv.at[step, r])
        total = ys[step, g].astype(F32)
        for r in range(1, G):
            total = total + yr[step, r].astype(F32)
        yg[step, g] = total.astype(BF16)
        for p in range(G - 1):
            r = hop(p, G)
            pltpu.make_async_remote_copy(
                src_ref=yg.at[step, g],
                dst_ref=yg.at[step, g],
                send_sem=yg_send.at[step],
                recv_sem=yg_recv.at[step, r],
                device_id=at_g(r),
                device_id_type=MESH,
            ).start()

    def update_ngrams(step, out):
        for r in range(1, G):
            settle(yg.at[step, (g + G - r) % G], yg_recv.at[step, r])
        for k in range(G):
            at = slice(k * piece, (k + 1) * piece)
            out[at, :] = v32[at, :] - ngram_rate * yg[step, k].astype(F32)

    def middle():
        update_ngrams(0, v32)
        v16[...] = v32[...].astype(BF16)

    gather_documents(0, lambda: None)

    @pl.loop(0, CHUNKS)
    def _(ch):
        find_errors(ch)
        send_documents(0, ch)

    send_ngrams(0)
    reduce_plane(0)
    reduce_ngrams(0)
    update_documents(0)

    gather_documents(1, middle)

    @pl.loop(0, CHUNKS)
    def _(ch):
        find_errors(ch)

    send_ngrams(1)

    @pl.loop(0, CHUNKS)
    def _(ch):
        send_documents(1, ch)

    reduce_plane(1)
    reduce_ngrams(1)
    update_documents(1)

    top = own32[0:4, :]
    bottom = own32[4:8, :]
    swap_out[1] = jnp.where(is_low, bottom, top)
    last_swap = swap(1)
    last_swap.start()
    kept = jnp.where(is_low, top, bottom)
    last_swap.wait()
    came = swap_in[1]
    doc_out[:, :half] = jnp.where(is_low, kept, came)
    doc_out[:, half:] = jnp.where(is_low, came, kept)

    update_ngrams(1, ngram_out)

    for step in range(2):
        settle(gath.at[step, 0 : Z - 1, 0], agz_send.at[step])
        settle(gath.at[step, :, 0 : Q - 1], agx_send.at[step])
        settle(xs.at[step, 0 : Q - 1], rsx_send.at[step])
        settle(zs.at[step, 0 : Z - 1], rsz_send.at[step])
        settle(ys.at[step, 0 : G - 1], ys_send.at[step])
        settle(yg.at[step, 0 : G - 1], yg_send.at[step])


def shards(doc_factors, ngram_factors, block_docs, block_ngrams, block_counts, pmi, weights):
    tiles = pmi.reshape(pmi.shape[2:])
    scales = weights.reshape(weights.shape[2:])
    shard_count = lax.axis_size("col")
    G = lax.axis_size("grp")
    Q = PLANE
    Z = shard_count // Q
    width = doc_factors.shape[1]
    half = width // 2
    ngrams = ngram_factors.shape[0]
    doc_total = doc_factors.shape[0] * shard_count * G
    ngram_total = ngrams * shard_count
    doc_base = math.sqrt(ngram_total) + 1.5 * math.sqrt(width)
    ngram_base = math.sqrt(doc_total) + 1.5 * math.sqrt(width)
    doc_rate = 100.0 / (doc_base * doc_base)
    ngram_rate = 100.0 / (ngram_base * ngram_base)
    docs = doc_factors.shape[0] * shard_count
    piece = ngrams // G
    vmem = pl.BlockSpec(memory_space=pltpu.VMEM)
    smem = pl.BlockSpec(memory_space=pltpu.SMEM)
    hbm = pl.BlockSpec(memory_space=pl.ANY)
    dma = pltpu.SemaphoreType.DMA
    return tuple(
        pl.pallas_call(
            functools.partial(kernel, Z, Q, G, doc_rate, ngram_rate),
            out_shape=(
                jax.ShapeDtypeStruct(doc_factors.shape, F32),
                jax.ShapeDtypeStruct(ngram_factors.shape, F32),
            ),
            in_specs=[vmem, smem, smem, smem, hbm, hbm, hbm],
            out_specs=(vmem, vmem),
            scratch_shapes=[
                pltpu.VMEM((ngrams, width), F32),
                pltpu.VMEM(tiles.shape, BF16),
                pltpu.VMEM(scales.shape, BF16),
                pltpu.VMEM((ngrams, width), BF16),
                pltpu.VMEM((docs, width), BF16),
                pltpu.VMEM((docs, ngrams), BF16),
                pltpu.VMEM((docs, ngrams), BF16),
                pltpu.VMEM((docs, ngrams), BF16),
                pltpu.SMEM((tiles.shape[0],), jnp.int32),
                pltpu.VMEM((8, half), F32),
                pltpu.VMEM((2, 4, half), F32),
                pltpu.VMEM((2, 4, half), F32),
                pltpu.VMEM((2, Z, Q, 8, half), BF16),
                pltpu.VMEM((2, Q, Z, 8, half), BF16),
                pltpu.VMEM((2, Q, Z, 8, half), BF16),
                pltpu.VMEM((2, Z, 8, half), F32),
                pltpu.VMEM((2, Z, 8, half), BF16),
                pltpu.VMEM((2, Z, 8, half), BF16),
                pltpu.VMEM((2, G, piece, width), BF16),
                pltpu.VMEM((2, G, piece, width), BF16),
                pltpu.VMEM((2, G, piece, width), BF16),
                dma((3,)),
                dma((2,)),
                dma((2,)),
                dma((2,)),
                dma((2, Z)),
                dma((2,)),
                dma((2, Q)),
                dma((2,)),
                dma((2, CHUNKS, Q)),
                dma((2,)),
                dma((2, Z)),
                dma((2,)),
                dma((2, G)),
                dma((2,)),
                dma((2, G)),
            ],
            compiler_params=pltpu.CompilerParams(collective_id=0, has_side_effects=True),
            name="factorize",
        )(doc_factors, block_docs, block_ngrams, block_counts, ngram_factors, tiles, scales)
    )


def solution(mesh):
    return jax.shard_map(
        shards,
        mesh=mesh,
        in_specs=(
            P(("grp", "col"), None),
            P("col", None),
            P("grp", "col", None),
            P("grp", "col", None),
            P("grp", "col"),
            P("grp", "col", None, None, None),
            P("grp", "col", None, None, None),
        ),
        out_specs=(P(("grp", "col"), None), P("col", None)),
        check_vma=False,
    )
```

```python
import functools
import math

import jax
import jax.numpy as jnp
from jax import lax
from jax.experimental import pallas as pl
from jax.experimental.pallas import tpu as pltpu
from jax.sharding import PartitionSpec as P

MESH = pl.DeviceIdType.MESH
F32 = jnp.float32
BF16 = jnp.bfloat16
CORES = 2
PLANE = 8
CHUNKS = 4
PARTS = 1
NT = (((1,), (1,)), ((), ()))
TN = (((0,), (0,)), ((), ()))


def hop(p, n):
    return n // 2 + ((p + 1) // 2) * (1 - 2 * (p % 2))


def kernel(
    Z,
    Q,
    G,
    doc_rate,
    ngram_rate,
    doc_hbm,
    docs_hbm,
    ngrams_hbm,
    count_hbm,
    ngram_hbm,
    pmi_hbm,
    weights_hbm,
    doc_out,
    ngram_now,
    ngram_grad,
    doc_ref,
    docs_ref,
    ngrams_ref,
    count_ref,
    v32,
    tiles,
    scales,
    v16,
    u16,
    u32,
    dense_p,
    dense_w,
    err,
    slot_of,
    own32,
    swap_out,
    swap_in,
    given,
    gath,
    xs,
    xr,
    rsum,
    zs,
    zr,
    ys,
    yr,
    yg,
    load_sem,
    swap_send,
    swap_recv,
    agz_send,
    agz_recv,
    agx_send,
    agx_recv,
    rsx_send,
    rsx_recv,
    rsz_send,
    rsz_recv,
    ys_send,
    ys_recv,
    yg_send,
    yg_recv,
):
    X = Q // CORES
    own_rows = doc_ref.shape[0]
    rows = 8 * X
    per = Z // CHUNKS
    chunk_rows = per * rows
    half = doc_ref.shape[1] // 2
    nslots, block_rows, block_cols = tiles.shape
    nnb = v32.shape[0] // block_cols
    per_block = block_rows // rows
    piece = v32.shape[0] // G
    part = piece // PARTS

    g = lax.axis_index("grp")
    col = lax.axis_index("col")
    z = col // Q
    q = col % Q
    core = q % CORES
    partner = q + 1 - 2 * core

    def at_z(dz):
        return {"col": ((z + dz) % Z) * Q + q}

    def at_q(r):
        return {"col": z * Q + (q + r) % Q}

    def at_g(r):
        return {"grp": (g + r) % G}

    barrier = pltpu.get_barrier_semaphore()

    @pl.loop(0, Z - 1)
    def _(p):
        pl.semaphore_signal(barrier, inc=1, device_id=at_z(hop(p, Z)), device_id_type=MESH)

    @pl.loop(1, Q)
    def _(r):
        pl.semaphore_signal(barrier, inc=1, device_id=at_q(r), device_id_type=MESH)

    @pl.loop(1, G)
    def _(r):
        pl.semaphore_signal(barrier, inc=1, device_id=at_g(r), device_id_type=MESH)

    pairs = (
        (docs_hbm, docs_ref),
        (ngrams_hbm, ngrams_ref),
        (count_hbm, count_ref),
        (doc_hbm, doc_ref),
        (ngram_hbm, v32),
        (pmi_hbm, tiles),
        (weights_hbm, scales),
    )
    loads = [
        pltpu.make_async_copy(source, target, load_sem.at[i])
        for i, (source, target) in enumerate(pairs)
    ]
    for load in loads:
        load.start()
    for load in loads[:4]:
        load.wait()

    is_low = core == 0
    low = doc_ref[:, :half]
    high = doc_ref[:, half:]
    mine = jnp.where(is_low, low, high)
    swap_out[0] = jnp.where(is_low, high, low)
    given[Z - 1, q] = doc_ref[...].astype(BF16)

    @pl.loop(0, nslots)
    def _(pair):
        found = jnp.int32(0)
        for k in range(nslots):
            name = docs_ref[0, 0, k] * nnb + ngrams_ref[0, 0, k]
            found = jnp.maximum(found, jnp.where(name == pair, k, 0))
        slot_of[pair] = found

    count = count_ref[0, 0]
    for load in loads[4:]:
        load.wait()

    v16[...] = v32[...].astype(BF16)

    @pl.loop(0, Z)
    def _(p):
        zd = (z + Z - hop(p, Z)) % Z
        block = zd // per_block
        first = pl.multiple_of((zd % per_block) * rows, rows)
        to = pl.multiple_of(p * rows, rows)
        for n in range(nnb):
            k = slot_of[block * nnb + n]
            lanes = slice(n * block_cols, (n + 1) * block_cols)
            live = jnp.where(k < count, 1.0, 0.0).astype(F32)
            dense_p[pl.ds(to, rows), lanes] = tiles[k, pl.ds(first, rows), :]
            dense_w[pl.ds(to, rows), lanes] = (
                live * scales[k, pl.ds(first, rows), :].astype(F32)
            ).astype(BF16)

    pl.semaphore_wait(barrier, Z + Q + G - 3)

    def swap(turn):
        return pltpu.make_async_remote_copy(
            src_ref=swap_out.at[turn],
            dst_ref=swap_in.at[turn],
            send_sem=swap_send.at[turn],
            recv_sem=swap_recv.at[turn],
            device_id={"col": z * Q + partner},
            device_id_type=MESH,
        )

    def settle(ref, sem):
        pltpu.make_async_copy(ref, ref, sem).wait()

    groups = [(Z - 1, Z)]
    while groups[-1][0] > 0:
        groups.append((max(0, groups[-1][0] - 4), groups[-1][0]))

    def gather_documents(step, here, between, filler):
        @pl.loop(0, Z - 1)
        def _(p):
            pltpu.make_async_remote_copy(
                src_ref=here.at[Z - 1, q],
                dst_ref=here.at[p, q],
                send_sem=agz_send.at[step],
                recv_sem=agz_recv.at[step, p],
                device_id=at_z(hop(p, Z)),
                device_id_type=MESH,
            ).start()

        between()
        for low_p, high_p in groups:
            if high_p < Z:
                for p in range(low_p, high_p):
                    settle(here.at[p, q], agz_recv.at[step, p])

            @pl.loop(1, Q)
            def _(r):
                pltpu.make_async_remote_copy(
                    src_ref=here.at[low_p:high_p, q],
                    dst_ref=here.at[low_p:high_p, q],
                    send_sem=agx_send.at[step],
                    recv_sem=agx_recv.at[step, r],
                    device_id=at_q(r),
                    device_id_type=MESH,
                ).start()

        filler()

        @pl.loop(1, Q)
        def _(r):
            settle(here.at[:, 0], agx_recv.at[step, r])

    def place_given():
        @pl.loop(0, Z)
        def _(p):
            to = pl.multiple_of(p * rows, rows)
            for k in range(Q):
                u32[p, k * own_rows : (k + 1) * own_rows, :] = given[p, k].astype(F32)
            u16[pl.ds(to, rows), :] = u32[p].astype(BF16)

    def place_gathered():
        @pl.loop(0, Z)
        def _(p):
            to = pl.multiple_of(p * rows, rows)
            for c in range(CORES):
                parts = [gath[p, x * CORES + c].astype(F32) for x in range(X)]
                u16[pl.ds(to, rows), c * half : (c + 1) * half] = jnp.concatenate(
                    parts, axis=0
                ).astype(BF16)

    def find_errors(ch):
        at = pl.ds(pl.multiple_of(ch * chunk_rows, chunk_rows), chunk_rows)
        scores = lax.dot_general(u16[at, :], v16[...], NT, preferred_element_type=F32)
        err[at, :] = (
            dense_w[at, :].astype(F32) * (scores - dense_p[at, :].astype(F32))
        ).astype(BF16)

    def send_documents(step, ch):
        at = pl.ds(pl.multiple_of(ch * chunk_rows, chunk_rows), chunk_rows)
        grad = jnp.dot(err[at, :], v16[...], preferred_element_type=F32)
        for k in range(per):
            for x in range(X):
                for c in range(CORES):
                    top = k * rows + x * 8
                    xs[step, x * CORES + c, ch * per + k] = grad[
                        top : top + 8, c * half : (c + 1) * half
                    ].astype(BF16)
        for r in range(1, Q):
            pltpu.make_async_remote_copy(
                src_ref=xs.at[step, (q + r) % Q, pl.ds(ch * per, per)],
                dst_ref=xr.at[step, r, pl.ds(ch * per, per)],
                send_sem=rsx_send.at[step],
                recv_sem=rsx_recv.at[step, ch, r],
                device_id=at_q(r),
                device_id_type=MESH,
            ).start()

    def send_ngrams(step):
        pieces = block_cols // piece

        def send(h, target, r):
            pltpu.make_async_remote_copy(
                src_ref=ys.at[step, h, target],
                dst_ref=yr.at[step, h, r],
                send_sem=ys_send.at[step],
                recv_sem=ys_recv.at[step, h, r],
                device_id={"grp": target},
                device_id_type=MESH,
            ).start()

        for n in range(nnb):
            grad = lax.dot_general(
                err[:, n * block_cols : (n + 1) * block_cols],
                u16[...],
                TN,
                preferred_element_type=F32,
            )
            for k in range(pieces):
                for h in range(PARTS):
                    top = k * piece + h * part
                    ys[step, h, n * pieces + k] = grad[top : top + part, :].astype(BF16)
            for k in range(pieces):
                target = n * pieces + k
                r = (target + G - g) % G

                @pl.when(r > 0)
                def _():
                    send(0, target, r)

        for h in range(1, PARTS):

            @pl.loop(0, G - 1)
            def _(p):
                r = hop(p, G)
                send(h, (g + r) % G, r)

    def reduce_plane(step):
        @pl.loop(0, CHUNKS)
        def _(ch):
            at = pl.ds(ch * per, per)
            total = xs[step, q, at].astype(F32)
            for r in range(1, Q):
                settle(xr.at[step, r, at], rsx_recv.at[step, ch, r])
            for r in range(1, Q):
                total = total + xr[step, r, at].astype(F32)
            rsum[step, at] = total
            zs[step, at] = total.astype(BF16)

            @pl.loop(0, per)
            def _(k):
                p = ch * per + k

                @pl.when(p < Z - 1)
                def _():
                    pltpu.make_async_remote_copy(
                        src_ref=zs.at[step, p],
                        dst_ref=zr.at[step, p],
                        send_sem=rsz_send.at[step],
                        recv_sem=rsz_recv.at[step, p],
                        device_id=at_z(Z - hop(p, Z)),
                        device_id_type=MESH,
                    ).start()

    def update_documents(step):
        total = rsum[step, Z - 1]
        for p in range(Z - 1):
            settle(zr.at[step, p], rsz_recv.at[step, p])
        for p in range(Z - 1):
            total = total + zr[step, p].astype(F32)
        own32[...] = own32[...] - doc_rate * total

    def reduce_ngrams(step):
        for h in range(PARTS):
            for r in range(1, G):
                settle(yr.at[step, h, r], ys_recv.at[step, h, r])
            total = ys[step, h, g].astype(F32)
            for r in range(1, G):
                total = total + yr[step, h, r].astype(F32)
            yg[step, h, g] = total.astype(BF16)

            @pl.loop(0, G - 1)
            def _(p):
                r = hop(p, G)
                pltpu.make_async_remote_copy(
                    src_ref=yg.at[step, h, g],
                    dst_ref=yg.at[step, h, g],
                    send_sem=yg_send.at[step],
                    recv_sem=yg_recv.at[step, h, r],
                    device_id=at_g(r),
                    device_id_type=MESH,
                ).start()

    def await_ngrams(step):
        for h in range(PARTS):
            for r in range(1, G):
                settle(yg.at[step, h, (g + G - r) % G], yg_recv.at[step, h, r])

    keep_ngrams = pltpu.make_async_copy(v32, ngram_now, load_sem.at[0])

    def middle():
        await_ngrams(0)
        for k in range(G):
            for h in range(PARTS):
                at = slice(k * piece + h * part, k * piece + (h + 1) * part)
                now = v32[at, :] - ngram_rate * yg[0, h, k].astype(F32)
                v32[at, :] = now
                v16[at, :] = now.astype(BF16)

    first_swap = swap(0)
    gather_documents(0, given, first_swap.start, lambda: None)
    place_given()

    @pl.loop(0, CHUNKS)
    def _(ch):
        find_errors(ch)
        send_documents(0, ch)

    send_ngrams(0)
    first_swap.wait()
    other = swap_in[0]
    own32[0:4, :] = jnp.where(is_low, mine, other)
    own32[4:8, :] = jnp.where(is_low, other, mine)
    reduce_plane(0)
    reduce_ngrams(0)
    update_documents(0)

    gath[Z - 1, q] = own32[...].astype(BF16)
    gather_documents(1, gath, lambda: None, middle)
    keep_ngrams.start()
    place_gathered()

    @pl.loop(0, CHUNKS)
    def _(ch):
        find_errors(ch)

    send_ngrams(1)

    @pl.loop(0, CHUNKS)
    def _(ch):
        send_documents(1, ch)

    reduce_plane(1)
    reduce_ngrams(1)
    update_documents(1)

    top = own32[0:4, :]
    bottom = own32[4:8, :]
    swap_out[1] = jnp.where(is_low, bottom, top)
    last_swap = swap(1)
    last_swap.start()
    kept = jnp.where(is_low, top, bottom)
    last_swap.wait()
    came = swap_in[1]
    doc_out[:, :half] = jnp.where(is_low, kept, came)
    doc_out[:, half:] = jnp.where(is_low, came, kept)

    for step, here in enumerate((given, gath)):
        settle(here.at[0 : Z - 1, 0], agz_send.at[step])
        settle(here.at[:, 0 : Q - 1], agx_send.at[step])
        settle(xs.at[step, 0 : Q - 1], rsx_send.at[step])
        settle(zs.at[step, 0 : Z - 1], rsz_send.at[step])
        settle(ys.at[step, :, 0 : G - 1], ys_send.at[step])
    settle(yg.at[0, :, 0 : G - 1], yg_send.at[0])
    keep_ngrams.wait()

    await_ngrams(1)
    last = pltpu.make_async_copy(yg.at[1], ngram_grad, load_sem.at[1])
    last.start()
    settle(yg.at[1, :, 0 : G - 1], yg_send.at[1])
    last.wait()


def finish(ngram_rate, doc_ref, ngram_ref, grad_ref, doc_out, ngram_out):
    doc_out[...] = doc_ref[...]
    parts, groups, part, width = grad_ref.shape
    for k in range(groups):
        for h in range(parts):
            top = (k * parts + h) * part
            at = slice(top, top + part)
            ngram_out[at, :] = ngram_ref[at, :] - ngram_rate * grad_ref[h, k].astype(F32)


def shards(doc_factors, ngram_factors, block_docs, block_ngrams, block_counts, pmi, weights):
    tiles = pmi.reshape(pmi.shape[2:])
    scales = weights.reshape(weights.shape[2:])
    shard_count = lax.axis_size("col")
    G = lax.axis_size("grp")
    Q = PLANE
    Z = shard_count // Q
    width = doc_factors.shape[1]
    half = width // 2
    ngrams = ngram_factors.shape[0]
    doc_total = doc_factors.shape[0] * shard_count * G
    ngram_total = ngrams * shard_count
    doc_base = math.sqrt(ngram_total) + 1.5 * math.sqrt(width)
    ngram_base = math.sqrt(doc_total) + 1.5 * math.sqrt(width)
    doc_rate = 100.0 / (doc_base * doc_base)
    ngram_rate = 100.0 / (ngram_base * ngram_base)
    docs = doc_factors.shape[0] * shard_count
    piece = ngrams // G
    vmem = pl.BlockSpec(memory_space=pltpu.VMEM)
    hbm = pl.BlockSpec(memory_space=pl.ANY)
    dma = pltpu.SemaphoreType.DMA
    doc_out, ngram_now, ngram_grad = pl.pallas_call(
        functools.partial(kernel, Z, Q, G, doc_rate, ngram_rate),
        out_shape=(
            jax.ShapeDtypeStruct(doc_factors.shape, F32),
            pltpu.VMEM(ngram_factors.shape, F32),
            pltpu.VMEM((PARTS, G, piece // PARTS, width), BF16),
        ),
        in_specs=[hbm] * 7,
        out_specs=(vmem, vmem, vmem),
        scratch_shapes=[
            pltpu.VMEM(doc_factors.shape, F32),
            pltpu.SMEM(block_docs.shape, jnp.int32),
            pltpu.SMEM(block_ngrams.shape, jnp.int32),
            pltpu.SMEM(block_counts.shape, jnp.int32),
            pltpu.VMEM((ngrams, width), F32),
            pltpu.VMEM(tiles.shape, BF16),
            pltpu.VMEM(scales.shape, BF16),
            pltpu.VMEM((ngrams, width), BF16),
            pltpu.VMEM((docs, width), BF16),
            pltpu.VMEM((Z, docs // Z, width), F32),
            pltpu.VMEM((docs, ngrams), BF16),
            pltpu.VMEM((docs, ngrams), BF16),
            pltpu.VMEM((docs, ngrams), BF16),
            pltpu.SMEM((tiles.shape[0],), jnp.int32),
            pltpu.VMEM((8, half), F32),
            pltpu.VMEM((2, 4, half), F32),
            pltpu.VMEM((2, 4, half), F32),
            pltpu.VMEM((Z, Q, doc_factors.shape[0], width), BF16),
            pltpu.VMEM((Z, Q, 8, half), BF16),
            pltpu.VMEM((2, Q, Z, 8, half), BF16),
            pltpu.VMEM((2, Q, Z, 8, half), BF16),
            pltpu.VMEM((2, Z, 8, half), F32),
            pltpu.VMEM((2, Z, 8, half), BF16),
            pltpu.VMEM((2, Z, 8, half), BF16),
            pltpu.VMEM((2, PARTS, G, piece // PARTS, width), BF16),
            pltpu.VMEM((2, PARTS, G, piece // PARTS, width), BF16),
            pltpu.VMEM((2, PARTS, G, piece // PARTS, width), BF16),
            dma((7,)),
            dma((2,)),
            dma((2,)),
            dma((2,)),
            dma((2, Z)),
            dma((2,)),
            dma((2, Q)),
            dma((2,)),
            dma((2, CHUNKS, Q)),
            dma((2,)),
            dma((2, Z)),
            dma((2,)),
            dma((2, PARTS, G)),
            dma((2,)),
            dma((2, PARTS, G)),
        ],
        compiler_params=pltpu.CompilerParams(collective_id=0, has_side_effects=True),
        name="factorize",
    )(doc_factors, block_docs, block_ngrams, block_counts, ngram_factors, tiles, scales)
    return tuple(
        pl.pallas_call(
            functools.partial(finish, ngram_rate),
            out_shape=(
                jax.ShapeDtypeStruct(doc_factors.shape, F32),
                jax.ShapeDtypeStruct(ngram_factors.shape, F32),
            ),
            in_specs=[vmem] * 3,
            out_specs=(vmem, vmem),
            name="finish",
        )(
            doc_out,
            pltpu.with_memory_space_constraint(ngram_now, pltpu.VMEM),
            pltpu.with_memory_space_constraint(ngram_grad, pltpu.VMEM),
        )
    )


def solution(mesh):
    return jax.shard_map(
        shards,
        mesh=mesh,
        in_specs=(
            P(("grp", "col"), None),
            P("col", None),
            P("grp", "col", None),
            P("grp", "col", None),
            P("grp", "col"),
            P("grp", "col", None, None, None),
            P("grp", "col", None, None, None),
        ),
        out_specs=(P(("grp", "col"), None), P("col", None)),
        check_vma=False,
    )
```

```python
import functools
import math

import jax
import jax.numpy as jnp
from jax import lax
from jax.experimental import pallas as pl
from jax.experimental.pallas import tpu as pltpu
from jax.sharding import PartitionSpec as P

MESH = pl.DeviceIdType.MESH
F32 = jnp.float32
BF16 = jnp.bfloat16
CORES = 2
PLANE = 8
CHUNKS = 4
PARTS = 1
NT = (((1,), (1,)), ((), ()))
TN = (((0,), (0,)), ((), ()))


def hop(p, n):
    return n // 2 + ((p + 1) // 2) * (1 - 2 * (p % 2))


def kernel(
    Z,
    Q,
    G,
    doc_rate,
    ngram_rate,
    doc_hbm,
    docs_hbm,
    ngrams_hbm,
    count_hbm,
    ngram_hbm,
    pmi_hbm,
    weights_hbm,
    doc_out,
    ngram_now,
    ngram_grad,
    doc_ref,
    docs_ref,
    ngrams_ref,
    count_ref,
    v32,
    tiles,
    scales,
    v16,
    u16,
    u32,
    dense_p,
    dense_w,
    err,
    slot_of,
    own32,
    swap_out,
    swap_in,
    given,
    gath,
    xs,
    xr,
    rsum,
    zs,
    zr,
    ys,
    yr,
    yg,
    load_sem,
    swap_send,
    swap_recv,
    agz_send,
    agz_recv,
    agx_send,
    agx_recv,
    rsx_send,
    rsx_recv,
    rsz_send,
    rsz_recv,
    ys_send,
    ys_recv,
    yg_send,
    yg_recv,
):
    X = Q // CORES
    own_rows = doc_ref.shape[0]
    rows = 8 * X
    per = Z // CHUNKS
    chunk_rows = per * rows
    half = doc_ref.shape[1] // 2
    nslots, block_rows, block_cols = tiles.shape
    nnb = v32.shape[0] // block_cols
    per_block = block_rows // rows
    piece = v32.shape[0] // G
    part = piece // PARTS

    g = lax.axis_index("grp")
    col = lax.axis_index("col")
    z = col // Q
    q = col % Q
    core = q % CORES
    partner = q + 1 - 2 * core

    def at_z(dz):
        return {"col": ((z + dz) % Z) * Q + q}

    def at_q(r):
        return {"col": z * Q + (q + r) % Q}

    def at_g(r):
        return {"grp": (g + r) % G}

    barrier = pltpu.get_barrier_semaphore()

    @pl.loop(0, Z - 1)
    def _(p):
        pl.semaphore_signal(barrier, inc=1, device_id=at_z(hop(p, Z)), device_id_type=MESH)

    @pl.loop(1, Q)
    def _(r):
        pl.semaphore_signal(barrier, inc=1, device_id=at_q(r), device_id_type=MESH)

    @pl.loop(1, G)
    def _(r):
        pl.semaphore_signal(barrier, inc=1, device_id=at_g(r), device_id_type=MESH)

    pairs = (
        (docs_hbm, docs_ref),
        (ngrams_hbm, ngrams_ref),
        (count_hbm, count_ref),
        (doc_hbm, doc_ref),
        (ngram_hbm, v32),
        (pmi_hbm, tiles),
        (weights_hbm, scales),
    )
    loads = [
        pltpu.make_async_copy(source, target, load_sem.at[i])
        for i, (source, target) in enumerate(pairs)
    ]
    for load in loads:
        load.start()
    for load in loads[:4]:
        load.wait()

    is_low = core == 0
    low = doc_ref[:, :half]
    high = doc_ref[:, half:]
    mine = jnp.where(is_low, low, high)
    swap_out[0] = jnp.where(is_low, high, low)
    given[Z - 1, q] = doc_ref[...].astype(BF16)

    @pl.loop(0, nslots)
    def _(pair):
        found = jnp.int32(0)
        for k in range(nslots):
            name = docs_ref[0, 0, k] * nnb + ngrams_ref[0, 0, k]
            found = jnp.maximum(found, jnp.where(name == pair, k, 0))
        slot_of[pair] = found

    count = count_ref[0, 0]
    for load in loads[4:]:
        load.wait()

    v16[...] = v32[...].astype(BF16)

    @pl.loop(0, Z)
    def _(p):
        zd = (z + Z - hop(p, Z)) % Z
        block = zd // per_block
        first = pl.multiple_of((zd % per_block) * rows, rows)
        to = pl.multiple_of(p * rows, rows)
        for n in range(nnb):
            k = slot_of[block * nnb + n]
            lanes = slice(n * block_cols, (n + 1) * block_cols)
            live = jnp.where(k < count, 1.0, 0.0).astype(F32)
            dense_p[pl.ds(to, rows), lanes] = tiles[k, pl.ds(first, rows), :]
            dense_w[pl.ds(to, rows), lanes] = (
                live * scales[k, pl.ds(first, rows), :].astype(F32)
            ).astype(BF16)

    pl.semaphore_wait(barrier, Z + Q + G - 3)

    def swap(turn):
        return pltpu.make_async_remote_copy(
            src_ref=swap_out.at[turn],
            dst_ref=swap_in.at[turn],
            send_sem=swap_send.at[turn],
            recv_sem=swap_recv.at[turn],
            device_id={"col": z * Q + partner},
            device_id_type=MESH,
        )

    def settle(ref, sem):
        pltpu.make_async_copy(ref, ref, sem).wait()

    groups = [(ch * per, (ch + 1) * per, ch) for ch in range(CHUNKS - 1, -1, -1)]

    def gather_documents(step, here, between, filler, place):
        @pl.loop(0, Z - 1)
        def _(p):
            pltpu.make_async_remote_copy(
                src_ref=here.at[Z - 1, q],
                dst_ref=here.at[p, q],
                send_sem=agz_send.at[step],
                recv_sem=agz_recv.at[step, p],
                device_id=at_z(hop(p, Z)),
                device_id_type=MESH,
            ).start()

        between()
        for low_p, high_p, ch in groups:
            for p in range(low_p, min(high_p, Z - 1)):
                settle(here.at[p, q], agz_recv.at[step, p])

            @pl.loop(0, Q - 1)
            def _(p):
                r = hop(p, Q)
                pltpu.make_async_remote_copy(
                    src_ref=here.at[low_p:high_p, q],
                    dst_ref=here.at[low_p:high_p, q],
                    send_sem=agx_send.at[step],
                    recv_sem=agx_recv.at[step, ch, r],
                    device_id=at_q(r),
                    device_id_type=MESH,
                ).start()

        filler()

        @pl.loop(0, CHUNKS)
        def _(i):
            ch = CHUNKS - 1 - i

            @pl.loop(1, Q)
            def _(r):
                settle(here.at[pl.ds(ch * per, per), 0], agx_recv.at[step, ch, r])

            for k in range(per):
                place(ch * per + k)
            find_errors(ch)

    def place_given(p):
        to = pl.multiple_of(p * rows, rows)
        for k in range(Q):
            u32[p, k * own_rows : (k + 1) * own_rows, :] = given[p, k].astype(F32)
        u16[pl.ds(to, rows), :] = u32[p].astype(BF16)

    def place_gathered(p):
        to = pl.multiple_of(p * rows, rows)
        for c in range(CORES):
            parts = [gath[p, x * CORES + c].astype(F32) for x in range(X)]
            u16[pl.ds(to, rows), c * half : (c + 1) * half] = jnp.concatenate(
                parts, axis=0
            ).astype(BF16)

    def find_errors(ch):
        at = pl.ds(pl.multiple_of(ch * chunk_rows, chunk_rows), chunk_rows)
        scores = lax.dot_general(u16[at, :], v16[...], NT, preferred_element_type=F32)
        err[at, :] = (
            dense_w[at, :].astype(F32) * (scores - dense_p[at, :].astype(F32))
        ).astype(BF16)

    def send_documents(step, ch):
        at = pl.ds(pl.multiple_of(ch * chunk_rows, chunk_rows), chunk_rows)
        grad = jnp.dot(err[at, :], v16[...], preferred_element_type=F32)
        for k in range(per):
            for x in range(X):
                for c in range(CORES):
                    top = k * rows + x * 8
                    xs[step, x * CORES + c, ch * per + k] = grad[
                        top : top + 8, c * half : (c + 1) * half
                    ].astype(BF16)
        for r in [hop(p, Q) for p in range(Q - 1)]:
            pltpu.make_async_remote_copy(
                src_ref=xs.at[step, (q + r) % Q, pl.ds(ch * per, per)],
                dst_ref=xr.at[step, r, pl.ds(ch * per, per)],
                send_sem=rsx_send.at[step],
                recv_sem=rsx_recv.at[step, ch, r],
                device_id=at_q(r),
                device_id_type=MESH,
            ).start()

    def send_ngrams(step):
        pieces = block_cols // piece

        def send(h, target, r):
            pltpu.make_async_remote_copy(
                src_ref=ys.at[step, h, target],
                dst_ref=yr.at[step, h, r],
                send_sem=ys_send.at[step],
                recv_sem=ys_recv.at[step, h, r],
                device_id={"grp": target},
                device_id_type=MESH,
            ).start()

        for n in range(nnb):
            grad = lax.dot_general(
                err[:, n * block_cols : (n + 1) * block_cols],
                u16[...],
                TN,
                preferred_element_type=F32,
            )
            for k in range(pieces):
                for h in range(PARTS):
                    top = k * piece + h * part
                    ys[step, h, n * pieces + k] = grad[top : top + part, :].astype(BF16)
            for k in range(pieces):
                target = n * pieces + k
                r = (target + G - g) % G

                @pl.when(r > 0)
                def _():
                    send(0, target, r)

        for h in range(1, PARTS):

            @pl.loop(0, G - 1)
            def _(p):
                r = hop(p, G)
                send(h, (g + r) % G, r)

    def reduce_plane(step):
        @pl.loop(0, CHUNKS)
        def _(ch):
            at = pl.ds(ch * per, per)
            total = xs[step, q, at].astype(F32)
            for r in range(1, Q):
                settle(xr.at[step, r, at], rsx_recv.at[step, ch, r])
            for r in range(1, Q):
                total = total + xr[step, r, at].astype(F32)
            rsum[step, at] = total
            zs[step, at] = total.astype(BF16)

            @pl.loop(0, per)
            def _(k):
                p = ch * per + k

                @pl.when(p < Z - 1)
                def _():
                    pltpu.make_async_remote_copy(
                        src_ref=zs.at[step, p],
                        dst_ref=zr.at[step, p],
                        send_sem=rsz_send.at[step],
                        recv_sem=rsz_recv.at[step, p],
                        device_id=at_z(Z - hop(p, Z)),
                        device_id_type=MESH,
                    ).start()

    def update_documents(step):
        total = rsum[step, Z - 1]
        for p in range(Z - 1):
            settle(zr.at[step, p], rsz_recv.at[step, p])
        for p in range(Z - 1):
            total = total + zr[step, p].astype(F32)
        own32[...] = own32[...] - doc_rate * total

    def reduce_ngrams(step):
        for h in range(PARTS):
            for r in range(1, G):
                settle(yr.at[step, h, r], ys_recv.at[step, h, r])
            total = ys[step, h, g].astype(F32)
            for r in range(1, G):
                total = total + yr[step, h, r].astype(F32)
            yg[step, h, g] = total.astype(BF16)

            @pl.loop(0, G - 1)
            def _(p):
                r = hop(p, G)
                pltpu.make_async_remote_copy(
                    src_ref=yg.at[step, h, g],
                    dst_ref=yg.at[step, h, g],
                    send_sem=yg_send.at[step],
                    recv_sem=yg_recv.at[step, h, r],
                    device_id=at_g(r),
                    device_id_type=MESH,
                ).start()

    def await_ngrams(step):
        for h in range(PARTS):
            for r in range(1, G):
                settle(yg.at[step, h, (g + G - r) % G], yg_recv.at[step, h, r])

    keep_ngrams = pltpu.make_async_copy(v32, ngram_now, load_sem.at[0])

    def middle():
        await_ngrams(0)
        for k in range(G):
            for h in range(PARTS):
                at = slice(k * piece + h * part, k * piece + (h + 1) * part)
                now = v32[at, :] - ngram_rate * yg[0, h, k].astype(F32)
                v32[at, :] = now
                v16[at, :] = now.astype(BF16)

    first_swap = swap(0)
    gather_documents(0, given, first_swap.start, lambda: None, place_given)

    @pl.loop(0, CHUNKS)
    def _(ch):
        send_documents(0, ch)

    send_ngrams(0)
    first_swap.wait()
    other = swap_in[0]
    own32[0:4, :] = jnp.where(is_low, mine, other)
    own32[4:8, :] = jnp.where(is_low, other, mine)
    reduce_plane(0)
    reduce_ngrams(0)
    update_documents(0)

    gath[Z - 1, q] = own32[...].astype(BF16)
    gather_documents(1, gath, lambda: None, middle, place_gathered)
    keep_ngrams.start()
    send_ngrams(1)

    @pl.loop(0, CHUNKS)
    def _(ch):
        send_documents(1, ch)

    reduce_plane(1)
    reduce_ngrams(1)
    update_documents(1)

    top = own32[0:4, :]
    bottom = own32[4:8, :]
    swap_out[1] = jnp.where(is_low, bottom, top)
    last_swap = swap(1)
    last_swap.start()
    kept = jnp.where(is_low, top, bottom)
    last_swap.wait()
    came = swap_in[1]
    doc_out[:, :half] = jnp.where(is_low, kept, came)
    doc_out[:, half:] = jnp.where(is_low, came, kept)

    for step, here in enumerate((given, gath)):
        settle(here.at[0 : Z - 1, 0], agz_send.at[step])
        settle(here.at[:, 0 : Q - 1], agx_send.at[step])
        settle(xs.at[step, 0 : Q - 1], rsx_send.at[step])
        settle(zs.at[step, 0 : Z - 1], rsz_send.at[step])
        settle(ys.at[step, :, 0 : G - 1], ys_send.at[step])
    settle(yg.at[0, :, 0 : G - 1], yg_send.at[0])
    keep_ngrams.wait()

    await_ngrams(1)
    last = pltpu.make_async_copy(yg.at[1], ngram_grad, load_sem.at[1])
    last.start()
    settle(yg.at[1, :, 0 : G - 1], yg_send.at[1])
    last.wait()


def finish(ngram_rate, doc_ref, ngram_ref, grad_ref, doc_out, ngram_out):
    doc_out[...] = doc_ref[...]
    parts, groups, part, width = grad_ref.shape
    for k in range(groups):
        for h in range(parts):
            top = (k * parts + h) * part
            at = slice(top, top + part)
            ngram_out[at, :] = ngram_ref[at, :] - ngram_rate * grad_ref[h, k].astype(F32)


def shards(doc_factors, ngram_factors, block_docs, block_ngrams, block_counts, pmi, weights):
    tiles = pmi.reshape(pmi.shape[2:])
    scales = weights.reshape(weights.shape[2:])
    shard_count = lax.axis_size("col")
    G = lax.axis_size("grp")
    Q = PLANE
    Z = shard_count // Q
    width = doc_factors.shape[1]
    half = width // 2
    ngrams = ngram_factors.shape[0]
    doc_total = doc_factors.shape[0] * shard_count * G
    ngram_total = ngrams * shard_count
    doc_base = math.sqrt(ngram_total) + 1.5 * math.sqrt(width)
    ngram_base = math.sqrt(doc_total) + 1.5 * math.sqrt(width)
    doc_rate = 100.0 / (doc_base * doc_base)
    ngram_rate = 100.0 / (ngram_base * ngram_base)
    docs = doc_factors.shape[0] * shard_count
    piece = ngrams // G
    vmem = pl.BlockSpec(memory_space=pltpu.VMEM)
    hbm = pl.BlockSpec(memory_space=pl.ANY)
    dma = pltpu.SemaphoreType.DMA
    doc_out, ngram_now, ngram_grad = pl.pallas_call(
        functools.partial(kernel, Z, Q, G, doc_rate, ngram_rate),
        out_shape=(
            jax.ShapeDtypeStruct(doc_factors.shape, F32),
            pltpu.VMEM(ngram_factors.shape, F32),
            pltpu.VMEM((PARTS, G, piece // PARTS, width), BF16),
        ),
        in_specs=[hbm] * 7,
        out_specs=(vmem, vmem, vmem),
        scratch_shapes=[
            pltpu.VMEM(doc_factors.shape, F32),
            pltpu.SMEM(block_docs.shape, jnp.int32),
            pltpu.SMEM(block_ngrams.shape, jnp.int32),
            pltpu.SMEM(block_counts.shape, jnp.int32),
            pltpu.VMEM((ngrams, width), F32),
            pltpu.VMEM(tiles.shape, BF16),
            pltpu.VMEM(scales.shape, BF16),
            pltpu.VMEM((ngrams, width), BF16),
            pltpu.VMEM((docs, width), BF16),
            pltpu.VMEM((Z, docs // Z, width), F32),
            pltpu.VMEM((docs, ngrams), BF16),
            pltpu.VMEM((docs, ngrams), BF16),
            pltpu.VMEM((docs, ngrams), BF16),
            pltpu.SMEM((tiles.shape[0],), jnp.int32),
            pltpu.VMEM((8, half), F32),
            pltpu.VMEM((2, 4, half), F32),
            pltpu.VMEM((2, 4, half), F32),
            pltpu.VMEM((Z, Q, doc_factors.shape[0], width), BF16),
            pltpu.VMEM((Z, Q, 8, half), BF16),
            pltpu.VMEM((2, Q, Z, 8, half), BF16),
            pltpu.VMEM((2, Q, Z, 8, half), BF16),
            pltpu.VMEM((2, Z, 8, half), F32),
            pltpu.VMEM((2, Z, 8, half), BF16),
            pltpu.VMEM((2, Z, 8, half), BF16),
            pltpu.VMEM((2, PARTS, G, piece // PARTS, width), BF16),
            pltpu.VMEM((2, PARTS, G, piece // PARTS, width), BF16),
            pltpu.VMEM((2, PARTS, G, piece // PARTS, width), BF16),
            dma((7,)),
            dma((2,)),
            dma((2,)),
            dma((2,)),
            dma((2, Z)),
            dma((2,)),
            dma((2, CHUNKS, Q)),
            dma((2,)),
            dma((2, CHUNKS, Q)),
            dma((2,)),
            dma((2, Z)),
            dma((2,)),
            dma((2, PARTS, G)),
            dma((2,)),
            dma((2, PARTS, G)),
        ],
        compiler_params=pltpu.CompilerParams(collective_id=0, has_side_effects=True),
        name="factorize",
    )(doc_factors, block_docs, block_ngrams, block_counts, ngram_factors, tiles, scales)
    return tuple(
        pl.pallas_call(
            functools.partial(finish, ngram_rate),
            out_shape=(
                jax.ShapeDtypeStruct(doc_factors.shape, F32),
                jax.ShapeDtypeStruct(ngram_factors.shape, F32),
            ),
            in_specs=[vmem] * 3,
            out_specs=(vmem, vmem),
            name="finish",
        )(
            doc_out,
            pltpu.with_memory_space_constraint(ngram_now, pltpu.VMEM),
            pltpu.with_memory_space_constraint(ngram_grad, pltpu.VMEM),
        )
    )


def solution(mesh):
    return jax.shard_map(
        shards,
        mesh=mesh,
        in_specs=(
            P(("grp", "col"), None),
            P("col", None),
            P("grp", "col", None),
            P("grp", "col", None),
            P("grp", "col"),
            P("grp", "col", None, None, None),
            P("grp", "col", None, None, None),
        ),
        out_specs=(P(("grp", "col"), None), P("col", None)),
        check_vma=False,
    )
```

```python
import functools
import math

import jax
import jax.numpy as jnp
from jax import lax
from jax.experimental import pallas as pl
from jax.experimental.pallas import tpu as pltpu
from jax.sharding import PartitionSpec as P

MESH = pl.DeviceIdType.MESH
F32 = jnp.float32
BF16 = jnp.bfloat16
CORES = 2
PLANE = 8
CHUNKS = 4
PARTS = 1
NT = (((1,), (1,)), ((), ()))
TN = (((0,), (0,)), ((), ()))


def hop(p, n):
    return n // 2 + ((p + 1) // 2) * (1 - 2 * (p % 2))


def kernel(
    Z,
    Q,
    G,
    doc_rate,
    ngram_rate,
    doc_hbm,
    docs_hbm,
    ngrams_hbm,
    count_hbm,
    ngram_hbm,
    pmi_hbm,
    weights_hbm,
    doc_out,
    ngram_now,
    ngram_grad,
    doc_ref,
    docs_ref,
    ngrams_ref,
    count_ref,
    v32,
    tiles,
    scales,
    v16,
    u16,
    u32,
    dense_p,
    dense_w,
    err,
    slot_of,
    own32,
    swap_out,
    swap_in,
    given,
    gath,
    xs,
    xr,
    rsum,
    zs,
    zr,
    ys,
    yr,
    yg,
    load_sem,
    swap_send,
    swap_recv,
    agz_send,
    agz_recv,
    agx_send,
    agx_recv,
    rsx_send,
    rsx_recv,
    rsz_send,
    rsz_recv,
    ys_send,
    ys_recv,
    yg_send,
    yg_recv,
):
    X = Q // CORES
    own_rows = doc_ref.shape[0]
    rows = 8 * X
    per = Z // CHUNKS
    chunk_rows = per * rows
    half = doc_ref.shape[1] // 2
    nslots, block_rows, block_cols = tiles.shape
    nnb = v32.shape[0] // block_cols
    per_block = block_rows // rows
    piece = v32.shape[0] // G
    part = piece // PARTS

    g = lax.axis_index("grp")
    col = lax.axis_index("col")
    z = col // Q
    q = col % Q
    core = q % CORES
    partner = q + 1 - 2 * core

    def at_z(dz):
        return {"col": ((z + dz) % Z) * Q + q}

    def at_q(r):
        return {"col": z * Q + (q + r) % Q}

    def at_g(r):
        return {"grp": (g + r) % G}

    plane = []
    for k in range(X):
        away = CORES * hop(k, X)
        if k < X - 1:
            plane.append(away)
        plane.append((away + Q + 1 - 2 * core) % Q)

    barrier = pltpu.get_barrier_semaphore()

    @pl.loop(0, Z - 1)
    def _(p):
        pl.semaphore_signal(barrier, inc=1, device_id=at_z(hop(p, Z)), device_id_type=MESH)

    @pl.loop(1, Q)
    def _(r):
        pl.semaphore_signal(barrier, inc=1, device_id=at_q(r), device_id_type=MESH)

    @pl.loop(1, G)
    def _(r):
        pl.semaphore_signal(barrier, inc=1, device_id=at_g(r), device_id_type=MESH)

    pairs = (
        (docs_hbm, docs_ref),
        (ngrams_hbm, ngrams_ref),
        (count_hbm, count_ref),
        (doc_hbm, doc_ref),
        (ngram_hbm, v32),
        (pmi_hbm, tiles),
        (weights_hbm, scales),
    )
    loads = [
        pltpu.make_async_copy(source, target, load_sem.at[i])
        for i, (source, target) in enumerate(pairs)
    ]
    for load in loads:
        load.start()
    for load in loads[:4]:
        load.wait()

    is_low = core == 0
    low = doc_ref[:, :half]
    high = doc_ref[:, half:]
    mine = jnp.where(is_low, low, high)
    swap_out[0] = jnp.where(is_low, high, low)
    given[Z - 1, q] = doc_ref[...].astype(BF16)

    @pl.loop(0, nslots)
    def _(pair):
        found = jnp.int32(0)
        for k in range(nslots):
            name = docs_ref[0, 0, k] * nnb + ngrams_ref[0, 0, k]
            found = jnp.maximum(found, jnp.where(name == pair, k, 0))
        slot_of[pair] = found

    count = count_ref[0, 0]
    for load in loads[4:]:
        load.wait()

    v16[...] = v32[...].astype(BF16)

    @pl.loop(0, Z)
    def _(p):
        zd = (z + Z - hop(p, Z)) % Z
        block = zd // per_block
        first = pl.multiple_of((zd % per_block) * rows, rows)
        to = pl.multiple_of(p * rows, rows)
        for n in range(nnb):
            k = slot_of[block * nnb + n]
            lanes = slice(n * block_cols, (n + 1) * block_cols)
            live = jnp.where(k < count, 1.0, 0.0).astype(F32)
            dense_p[pl.ds(to, rows), lanes] = tiles[k, pl.ds(first, rows), :]
            dense_w[pl.ds(to, rows), lanes] = (
                live * scales[k, pl.ds(first, rows), :].astype(F32)
            ).astype(BF16)

    pl.semaphore_wait(barrier, Z + Q + G - 3)

    def swap(turn):
        return pltpu.make_async_remote_copy(
            src_ref=swap_out.at[turn],
            dst_ref=swap_in.at[turn],
            send_sem=swap_send.at[turn],
            recv_sem=swap_recv.at[turn],
            device_id={"col": z * Q + partner},
            device_id_type=MESH,
        )

    def settle(ref, sem):
        pltpu.make_async_copy(ref, ref, sem).wait()

    groups = [(ch * per, (ch + 1) * per, ch) for ch in range(CHUNKS - 1, -1, -1)]

    def gather_documents(step, here, between, filler, place):
        @pl.loop(0, Z - 1)
        def _(p):
            pltpu.make_async_remote_copy(
                src_ref=here.at[Z - 1, q],
                dst_ref=here.at[p, q],
                send_sem=agz_send.at[step],
                recv_sem=agz_recv.at[step, p],
                device_id=at_z(hop(p, Z)),
                device_id_type=MESH,
            ).start()

        between()
        for low_p, high_p, ch in groups:
            for p in range(low_p, min(high_p, Z - 1)):
                settle(here.at[p, q], agz_recv.at[step, p])

            for r in plane:
                pltpu.make_async_remote_copy(
                    src_ref=here.at[low_p:high_p, q],
                    dst_ref=here.at[low_p:high_p, q],
                    send_sem=agx_send.at[step],
                    recv_sem=agx_recv.at[step, ch, r],
                    device_id=at_q(r),
                    device_id_type=MESH,
                ).start()

        filler()

        @pl.loop(0, CHUNKS)
        def _(i):
            ch = CHUNKS - 1 - i

            @pl.loop(1, Q)
            def _(r):
                settle(here.at[pl.ds(ch * per, per), 0], agx_recv.at[step, ch, r])

            for k in range(per):
                place(ch * per + k)
            find_errors(ch)

    def place_given(p):
        to = pl.multiple_of(p * rows, rows)
        for k in range(Q):
            u32[p, k * own_rows : (k + 1) * own_rows, :] = given[p, k].astype(F32)
        u16[pl.ds(to, rows), :] = u32[p].astype(BF16)

    def place_gathered(p):
        to = pl.multiple_of(p * rows, rows)
        for c in range(CORES):
            parts = [gath[p, x * CORES + c].astype(F32) for x in range(X)]
            u16[pl.ds(to, rows), c * half : (c + 1) * half] = jnp.concatenate(
                parts, axis=0
            ).astype(BF16)

    def find_errors(ch):
        at = pl.ds(pl.multiple_of(ch * chunk_rows, chunk_rows), chunk_rows)
        scores = lax.dot_general(u16[at, :], v16[...], NT, preferred_element_type=F32)
        err[at, :] = (
            dense_w[at, :].astype(F32) * (scores - dense_p[at, :].astype(F32))
        ).astype(BF16)

    def send_documents(step, ch):
        at = pl.ds(pl.multiple_of(ch * chunk_rows, chunk_rows), chunk_rows)
        grad = jnp.dot(err[at, :], v16[...], preferred_element_type=F32)
        for k in range(per):
            for x in range(X):
                for c in range(CORES):
                    top = k * rows + x * 8
                    xs[step, x * CORES + c, ch * per + k] = grad[
                        top : top + 8, c * half : (c + 1) * half
                    ].astype(BF16)
        for r in plane:
            pltpu.make_async_remote_copy(
                src_ref=xs.at[step, (q + r) % Q, pl.ds(ch * per, per)],
                dst_ref=xr.at[step, r, pl.ds(ch * per, per)],
                send_sem=rsx_send.at[step],
                recv_sem=rsx_recv.at[step, ch, r],
                device_id=at_q(r),
                device_id_type=MESH,
            ).start()

    def send_ngrams(step):
        pieces = block_cols // piece

        def send(h, target, r):
            pltpu.make_async_remote_copy(
                src_ref=ys.at[step, h, target],
                dst_ref=yr.at[step, h, r],
                send_sem=ys_send.at[step],
                recv_sem=ys_recv.at[step, h, r],
                device_id={"grp": target},
                device_id_type=MESH,
            ).start()

        for n in range(nnb):
            grad = lax.dot_general(
                err[:, n * block_cols : (n + 1) * block_cols],
                u16[...],
                TN,
                preferred_element_type=F32,
            )
            for k in range(pieces):
                for h in range(PARTS):
                    top = k * piece + h * part
                    ys[step, h, n * pieces + k] = grad[top : top + part, :].astype(BF16)
            for k in range(pieces):
                target = n * pieces + k
                r = (target + G - g) % G

                @pl.when(r > 0)
                def _():
                    send(0, target, r)

        for h in range(1, PARTS):

            @pl.loop(0, G - 1)
            def _(p):
                r = hop(p, G)
                send(h, (g + r) % G, r)

    def reduce_plane(step):
        @pl.loop(0, CHUNKS)
        def _(ch):
            at = pl.ds(ch * per, per)
            total = xs[step, q, at].astype(F32)
            for r in range(1, Q):
                settle(xr.at[step, r, at], rsx_recv.at[step, ch, r])
            for r in range(1, Q):
                total = total + xr[step, r, at].astype(F32)
            rsum[step, at] = total
            zs[step, at] = total.astype(BF16)

            @pl.loop(0, per)
            def _(k):
                p = ch * per + k

                @pl.when(p < Z - 1)
                def _():
                    pltpu.make_async_remote_copy(
                        src_ref=zs.at[step, p],
                        dst_ref=zr.at[step, p],
                        send_sem=rsz_send.at[step],
                        recv_sem=rsz_recv.at[step, p],
                        device_id=at_z(Z - hop(p, Z)),
                        device_id_type=MESH,
                    ).start()

    def update_documents(step):
        total = rsum[step, Z - 1]
        for p in range(Z - 1):
            settle(zr.at[step, p], rsz_recv.at[step, p])
        for p in range(Z - 1):
            total = total + zr[step, p].astype(F32)
        own32[...] = own32[...] - doc_rate * total

    def reduce_ngrams(step):
        for h in range(PARTS):
            for r in range(1, G):
                settle(yr.at[step, h, r], ys_recv.at[step, h, r])
            total = ys[step, h, g].astype(F32)
            for r in range(1, G):
                total = total + yr[step, h, r].astype(F32)
            yg[step, h, g] = total.astype(BF16)

            @pl.loop(0, G - 1)
            def _(p):
                r = hop(p, G)
                pltpu.make_async_remote_copy(
                    src_ref=yg.at[step, h, g],
                    dst_ref=yg.at[step, h, g],
                    send_sem=yg_send.at[step],
                    recv_sem=yg_recv.at[step, h, r],
                    device_id=at_g(r),
                    device_id_type=MESH,
                ).start()

    def await_ngrams(step):
        for h in range(PARTS):
            for r in range(1, G):
                settle(yg.at[step, h, (g + G - r) % G], yg_recv.at[step, h, r])

    keep_ngrams = pltpu.make_async_copy(v32, ngram_now, load_sem.at[0])

    def middle():
        await_ngrams(0)
        for k in range(G):
            for h in range(PARTS):
                at = slice(k * piece + h * part, k * piece + (h + 1) * part)
                now = v32[at, :] - ngram_rate * yg[0, h, k].astype(F32)
                v32[at, :] = now
                v16[at, :] = now.astype(BF16)

    first_swap = swap(0)
    gather_documents(0, given, first_swap.start, lambda: None, place_given)

    @pl.loop(0, CHUNKS)
    def _(ch):
        send_documents(0, ch)

    send_ngrams(0)
    first_swap.wait()
    other = swap_in[0]
    own32[0:4, :] = jnp.where(is_low, mine, other)
    own32[4:8, :] = jnp.where(is_low, other, mine)
    reduce_plane(0)
    reduce_ngrams(0)
    update_documents(0)

    gath[Z - 1, q] = own32[...].astype(BF16)
    gather_documents(1, gath, lambda: None, middle, place_gathered)
    keep_ngrams.start()
    send_ngrams(1)

    @pl.loop(0, CHUNKS)
    def _(ch):
        send_documents(1, ch)

    reduce_plane(1)
    reduce_ngrams(1)
    update_documents(1)

    top = own32[0:4, :]
    bottom = own32[4:8, :]
    swap_out[1] = jnp.where(is_low, bottom, top)
    last_swap = swap(1)
    last_swap.start()
    kept = jnp.where(is_low, top, bottom)
    last_swap.wait()
    came = swap_in[1]
    doc_out[:, :half] = jnp.where(is_low, kept, came)
    doc_out[:, half:] = jnp.where(is_low, came, kept)

    for step, here in enumerate((given, gath)):
        settle(here.at[0 : Z - 1, 0], agz_send.at[step])
        settle(here.at[:, 0 : Q - 1], agx_send.at[step])
        settle(xs.at[step, 0 : Q - 1], rsx_send.at[step])
        settle(zs.at[step, 0 : Z - 1], rsz_send.at[step])
        settle(ys.at[step, :, 0 : G - 1], ys_send.at[step])
    settle(yg.at[0, :, 0 : G - 1], yg_send.at[0])
    keep_ngrams.wait()

    await_ngrams(1)
    last = pltpu.make_async_copy(yg.at[1], ngram_grad, load_sem.at[1])
    last.start()
    settle(yg.at[1, :, 0 : G - 1], yg_send.at[1])
    last.wait()


def finish(ngram_rate, doc_ref, ngram_ref, grad_ref, doc_out, ngram_out):
    doc_out[...] = doc_ref[...]
    parts, groups, part, width = grad_ref.shape
    for k in range(groups):
        for h in range(parts):
            top = (k * parts + h) * part
            at = slice(top, top + part)
            ngram_out[at, :] = ngram_ref[at, :] - ngram_rate * grad_ref[h, k].astype(F32)


def shards(doc_factors, ngram_factors, block_docs, block_ngrams, block_counts, pmi, weights):
    tiles = pmi.reshape(pmi.shape[2:])
    scales = weights.reshape(weights.shape[2:])
    shard_count = lax.axis_size("col")
    G = lax.axis_size("grp")
    Q = PLANE
    Z = shard_count // Q
    width = doc_factors.shape[1]
    half = width // 2
    ngrams = ngram_factors.shape[0]
    doc_total = doc_factors.shape[0] * shard_count * G
    ngram_total = ngrams * shard_count
    doc_base = math.sqrt(ngram_total) + 1.5 * math.sqrt(width)
    ngram_base = math.sqrt(doc_total) + 1.5 * math.sqrt(width)
    doc_rate = 100.0 / (doc_base * doc_base)
    ngram_rate = 100.0 / (ngram_base * ngram_base)
    docs = doc_factors.shape[0] * shard_count
    piece = ngrams // G
    vmem = pl.BlockSpec(memory_space=pltpu.VMEM)
    hbm = pl.BlockSpec(memory_space=pl.ANY)
    dma = pltpu.SemaphoreType.DMA
    doc_out, ngram_now, ngram_grad = pl.pallas_call(
        functools.partial(kernel, Z, Q, G, doc_rate, ngram_rate),
        out_shape=(
            jax.ShapeDtypeStruct(doc_factors.shape, F32),
            pltpu.VMEM(ngram_factors.shape, F32),
            pltpu.VMEM((PARTS, G, piece // PARTS, width), BF16),
        ),
        in_specs=[hbm] * 7,
        out_specs=(vmem, vmem, vmem),
        scratch_shapes=[
            pltpu.VMEM(doc_factors.shape, F32),
            pltpu.SMEM(block_docs.shape, jnp.int32),
            pltpu.SMEM(block_ngrams.shape, jnp.int32),
            pltpu.SMEM(block_counts.shape, jnp.int32),
            pltpu.VMEM((ngrams, width), F32),
            pltpu.VMEM(tiles.shape, BF16),
            pltpu.VMEM(scales.shape, BF16),
            pltpu.VMEM((ngrams, width), BF16),
            pltpu.VMEM((docs, width), BF16),
            pltpu.VMEM((Z, docs // Z, width), F32),
            pltpu.VMEM((docs, ngrams), BF16),
            pltpu.VMEM((docs, ngrams), BF16),
            pltpu.VMEM((docs, ngrams), BF16),
            pltpu.SMEM((tiles.shape[0],), jnp.int32),
            pltpu.VMEM((8, half), F32),
            pltpu.VMEM((2, 4, half), F32),
            pltpu.VMEM((2, 4, half), F32),
            pltpu.VMEM((Z, Q, doc_factors.shape[0], width), BF16),
            pltpu.VMEM((Z, Q, 8, half), BF16),
            pltpu.VMEM((2, Q, Z, 8, half), BF16),
            pltpu.VMEM((2, Q, Z, 8, half), BF16),
            pltpu.VMEM((2, Z, 8, half), F32),
            pltpu.VMEM((2, Z, 8, half), BF16),
            pltpu.VMEM((2, Z, 8, half), BF16),
            pltpu.VMEM((2, PARTS, G, piece // PARTS, width), BF16),
            pltpu.VMEM((2, PARTS, G, piece // PARTS, width), BF16),
            pltpu.VMEM((2, PARTS, G, piece // PARTS, width), BF16),
            dma((7,)),
            dma((2,)),
            dma((2,)),
            dma((2,)),
            dma((2, Z)),
            dma((2,)),
            dma((2, CHUNKS, Q)),
            dma((2,)),
            dma((2, CHUNKS, Q)),
            dma((2,)),
            dma((2, Z)),
            dma((2,)),
            dma((2, PARTS, G)),
            dma((2,)),
            dma((2, PARTS, G)),
        ],
        compiler_params=pltpu.CompilerParams(collective_id=0, has_side_effects=True),
        name="factorize",
    )(doc_factors, block_docs, block_ngrams, block_counts, ngram_factors, tiles, scales)
    return tuple(
        pl.pallas_call(
            functools.partial(finish, ngram_rate),
            out_shape=(
                jax.ShapeDtypeStruct(doc_factors.shape, F32),
                jax.ShapeDtypeStruct(ngram_factors.shape, F32),
            ),
            in_specs=[vmem] * 3,
            out_specs=(vmem, vmem),
            name="finish",
        )(
            doc_out,
            pltpu.with_memory_space_constraint(ngram_now, pltpu.VMEM),
            pltpu.with_memory_space_constraint(ngram_grad, pltpu.VMEM),
        )
    )


def solution(mesh):
    return jax.shard_map(
        shards,
        mesh=mesh,
        in_specs=(
            P(("grp", "col"), None),
            P("col", None),
            P("grp", "col", None),
            P("grp", "col", None),
            P("grp", "col"),
            P("grp", "col", None, None, None),
            P("grp", "col", None, None, None),
        ),
        out_specs=(P(("grp", "col"), None), P("col", None)),
        check_vma=False,
    )
```
